32 devices in a mesh: row: 4 (over y, core), col: 8 (over z, x).
Axes of the slice: x: 2, y: 2, z: 4, core: 2. Of those that a mesh axis runs over, the one named last changes fastest.
Arguments:
- image: bfloat16 [1024, 1024], P(('col', 'row')), may hold values from -1 to 1
- text: bfloat16 [1024, 1024], P(('row', 'col')), may hold values from -1 to 1
- audio: bfloat16 [1024, 1024], P(('row', 'col')), may hold values from -1 to 1
Outputs:
- image_grad: float32 [1024, 1024], P(('col', 'row'))
- text_grad: float32 [1024, 1024], P(('row', 'col'))
- audio_grad: float32 [1024, 1024], P(('row', 'col'))
- loss: float32 [], replicated
The draws below stay inside these ranges and needn't reach their ends.
All inputs are finite; a program needn't handle non-finite values.
Results may differ from the reference program's by a relative error of at most 0.0063.
Values may be sent and summed in bfloat16 or wider, within the bound.
A program may use at most 64 MiB of HBM per device.

```python
import math
import jax
import jax.numpy as jnp
from jax import lax

E = 1024
BATCH = 1024


def common_rows(key):
    base_key = jax.random.fold_in(key, 7001)
    direction = jax.random.normal(jax.random.fold_in(base_key, 1), (BATCH, E), jnp.float32)
    return direction


def row_scales(own_key):
    lower, upper = (0.5, 2.0)
    logs = jax.random.uniform(jax.random.fold_in(own_key, 11), (BATCH, 1), jnp.float32, math.log(lower), math.log(upper))
    return jnp.exp(logs)


def paired_rows(key, stream):
    direction = common_rows(key)
    own_key = jax.random.fold_in(key, stream)
    mixing = jax.random.uniform(jax.random.fold_in(own_key, 5), (BATCH, 1), jnp.float32, 0.25, 0.85)
    own_noise = jax.random.normal(jax.random.fold_in(own_key, 6), (BATCH, E), jnp.float32)
    mixed = mixing * direction + jnp.sqrt(1.0 - mixing * mixing) * own_noise
    values = mixed * row_scales(own_key) * 0.03125
    return jnp.clip(values, -1.0, 1.0).astype(jnp.bfloat16)


def draw_image(key, part):
    direction = common_rows(key)
    own_key = jax.random.fold_in(key, 8101)
    values = direction * row_scales(own_key) * 0.03125
    return jnp.clip(values, -1.0, 1.0).astype(jnp.bfloat16)


def draw_text(key, part):
    return paired_rows(key, 8202)


def draw_audio(key, part):
    return paired_rows(key, 8303)


def setup_inputs(seed: int = 0) -> dict:
    splits = jax.random.split(jax.random.key(seed), 4)
    return {
        "image": draw_image(jax.random.fold_in(splits[3], 71), 0),
        "text": draw_text(jax.random.fold_in(splits[3], 71), 0),
        "audio": draw_audio(jax.random.fold_in(splits[3], 71), 0),
    }


logit_scale = 20.0
epsilon = 1e-06

def normalize(values):
    widened = values.astype(jnp.float32)
    radius = jnp.sqrt(lax.optimization_barrier(jnp.sum(widened * widened, axis=-1, keepdims=True)) + epsilon)
    return (widened / radius, radius)

def through_norm(grad_unit, unit, radius):
    inner = lax.optimization_barrier(jnp.sum(unit * grad_unit, axis=-1, keepdims=True))
    return (grad_unit - unit * inner) / radius

def scores(left, right):
    return logit_scale * lax.dot_general(left, right, (((1,), (1,)), ((), ())), preferred_element_type=jnp.float32)

def reference(image, text, audio):
    batch_size = image.shape[0]
    feature_width = image.shape[1]
    block_rows = min(512, batch_size)
    block_count = batch_size // block_rows
    image_unit, image_radius = normalize(image)
    text_unit, text_radius = normalize(text)
    audio_unit, audio_radius = normalize(audio)
    image_half = image_unit.astype(jnp.bfloat16)
    text_half = text_unit.astype(jnp.bfloat16)
    audio_half = audio_unit.astype(jnp.bfloat16)
    blocks = jnp.arange(block_count, dtype=jnp.int32)

    def first_pass(running, block_index):
        image_rows = lax.dynamic_slice_in_dim(image_half, block_index * block_rows, block_rows, 0)
        text_exp = jnp.exp(scores(image_rows, text_half) - logit_scale)
        audio_exp = jnp.exp(scores(image_rows, audio_half) - logit_scale)
        updated = (running[0] + lax.optimization_barrier(jnp.sum(text_exp, axis=0)), running[1] + lax.optimization_barrier(jnp.sum(audio_exp, axis=0)))
        return (updated, (lax.optimization_barrier(jnp.sum(text_exp, axis=1)), lax.optimization_barrier(jnp.sum(audio_exp, axis=1))))
    empty_sums = jnp.zeros((batch_size,), jnp.float32)
    (text_column, audio_column), (text_row, audio_row) = lax.scan(first_pass, (empty_sums, empty_sums), blocks)
    text_row = text_row.reshape(batch_size)
    audio_row = audio_row.reshape(batch_size)
    positions = jnp.arange(batch_size, dtype=jnp.int32)

    def second_pass(running, block_index):
        first_row = (block_index * block_rows).astype(jnp.int32)
        image_rows = lax.dynamic_slice_in_dim(image_half, first_row, block_rows, 0)
        diagonal = (first_row + jnp.arange(block_rows, dtype=jnp.int32))[:, None] == positions[None, :]
        twice_diagonal = jnp.where(diagonal, 2.0, 0.0).astype(jnp.float32)
        text_scores = scores(image_rows, text_half)
        audio_scores = scores(image_rows, audio_half)
        text_exp = jnp.exp(text_scores - logit_scale)
        audio_exp = jnp.exp(audio_scores - logit_scale)
        row_text = lax.dynamic_slice_in_dim(text_row, first_row, block_rows, 0)
        row_audio = lax.dynamic_slice_in_dim(audio_row, first_row, block_rows, 0)
        text_weights = (text_exp / row_text[:, None] + text_exp / text_column[None, :] - twice_diagonal).astype(jnp.bfloat16)
        audio_weights = (audio_exp / row_audio[:, None] + audio_exp / audio_column[None, :] - twice_diagonal).astype(jnp.bfloat16)
        image_part = logit_scale * (jnp.dot(text_weights, text_half, preferred_element_type=jnp.float32) + jnp.dot(audio_weights, audio_half, preferred_element_type=jnp.float32))
        text_acc = running[0] + lax.dot_general(text_weights, image_rows, (((0,), (0,)), ((), ())), preferred_element_type=jnp.float32)
        audio_acc = running[1] + lax.dot_general(audio_weights, image_rows, (((0,), (0,)), ((), ())), preferred_element_type=jnp.float32)
        diagonal_sum = running[2] + jnp.sum(jnp.where(diagonal, text_scores + audio_scores, 0.0))
        return ((text_acc, audio_acc, diagonal_sum), image_part)
    empty_grad = jnp.zeros((batch_size, feature_width), jnp.float32)
    (text_acc, audio_acc, diagonal_sum), image_part = lax.scan(second_pass, (empty_grad, empty_grad, jnp.zeros((), jnp.float32)), blocks)
    image_part = image_part.reshape(batch_size, feature_width)
    loss_sum = jnp.sum(jnp.log(text_row)) + jnp.sum(jnp.log(audio_row)) + jnp.sum(jnp.log(text_column)) + jnp.sum(jnp.log(audio_column)) - 2.0 * diagonal_sum
    loss = loss_sum / (4.0 * batch_size) + logit_scale
    return (through_norm(image_part, image_unit, image_radius), through_norm(logit_scale * text_acc, text_unit, text_radius), through_norm(logit_scale * audio_acc, audio_unit, audio_radius), loss)
```

```python
import functools

import jax
import jax.numpy as jnp
from jax import lax
from jax.experimental import pallas as pl
from jax.experimental.pallas import tpu as pltpu
from jax.sharding import PartitionSpec as P

MESH = pl.DeviceIdType.MESH
logit_scale = 20.0
epsilon = 1e-06


def inverse_radius(values):
    return lax.rsqrt(jnp.sum(values * values, axis=-1, keepdims=True) + epsilon)


def contract(left, right, left_dim, right_dim):
    return lax.dot_general(
        left, right, (((left_dim,), (right_dim,)), ((), ())), preferred_element_type=jnp.float32
    )


def loop(count, body):
    if count == 1:
        body(0)
    else:

        def step(index, carry):
            body(index)
            return carry

        lax.fori_loop(0, count, step, 0)


def kernel(
    R, C, n, F, G,
    image_ref, text_ref, audio_ref,
    image_out, text_out, audio_out, loss_out,
    img, pair, exp_ip, exp_pi, stat_c, stat_r, loss_c, loss_r,
    part_i, recv_i, part_p, recv_p, acc,
    img_s, img_r, pair_s, pair_r, sc_s, sc_r, sr_s, sr_r,
    lc_s, lc_r, lr_s, lr_r, pi_s, pi_r, pp_s, pp_r,
):
    r = lax.axis_index("row")
    c = lax.axis_index("col")
    B = C // G
    M = B * n
    H = R * n
    Q = 2 * H
    cols = [lax.rem(c + k, C) for k in range(1, C)]
    rows = [lax.rem(r + k, R) for k in range(1, R)]

    barrier = pltpu.get_barrier_semaphore()
    for p in cols:
        pl.semaphore_signal(barrier, inc=1, device_id=(r, p), device_id_type=MESH)
    for p in rows:
        pl.semaphore_signal(barrier, inc=1, device_id=(p, c), device_id_type=MESH)

    def to_col(src, dst, send, recv, p):
        return pltpu.make_async_remote_copy(
            src_ref=src, dst_ref=dst, send_sem=send.at[p], recv_sem=recv.at[c],
            device_id=(r, p), device_id_type=MESH,
        )

    def to_row(src, dst, send, recv, p):
        return pltpu.make_async_remote_copy(
            src_ref=src, dst_ref=dst, send_sem=send.at[p], recv_sem=recv.at[r],
            device_id=(p, c), device_id_type=MESH,
        )

    def from_col(dst, send, recv, p):
        pltpu.make_async_remote_copy(
            src_ref=dst, dst_ref=dst, send_sem=send.at[p], recv_sem=recv.at[p],
            device_id=(r, p), device_id_type=MESH,
        ).wait_recv()

    def from_row(dst, send, recv, p):
        pltpu.make_async_remote_copy(
            src_ref=dst, dst_ref=dst, send_sem=send.at[p], recv_sem=recv.at[p],
            device_id=(p, c), device_id_type=MESH,
        ).wait_recv()

    sent = []

    def go(copy):
        copy.start()
        sent.append(copy)

    x = image_ref[...].astype(jnp.float32)
    img[c] = (x * inverse_radius(x)).astype(jnp.bfloat16)
    x = text_ref[...].astype(jnp.float32)
    pair[0, r] = (x * inverse_radius(x)).astype(jnp.bfloat16)
    x = audio_ref[...].astype(jnp.float32)
    pair[1, r] = (x * inverse_radius(x)).astype(jnp.bfloat16)

    pl.semaphore_wait(barrier, C - 1 + R - 1)
    for p in rows:
        go(to_row(pair.at[:, r], pair.at[:, r], pair_s, pair_r, p))
    for p in cols:
        go(to_col(img.at[c], img.at[c], img_s, img_r, p))
    for p in rows:
        from_row(pair.at[:, p], pair_s, pair_r, p)
    for p in cols:
        from_col(img.at[p], img_s, img_r, p)

    def block_ids(count, shape, axis, stride, first):
        local = lax.broadcasted_iota(jnp.int32, shape, axis)
        return (lax.rem(lax.div(local, n), count) * stride + first) * n + lax.rem(local, n)

    col_sum = jnp.zeros((1, Q), jnp.float32)

    def exps(g):
        images = img[pl.ds(g * B, B)].reshape(M, F)
        pairs = pair[...].reshape(Q, F)
        s_pi = logit_scale * contract(pairs, images, 1, 1)
        image_id = block_ids(B, (1, M), 1, R, r + g * (B * R))
        pair_id = block_ids(R, (Q, 1), 0, C, c)
        diagonal = jnp.sum(jnp.where(image_id == pair_id, s_pi, 0.0), axis=0, keepdims=True)
        e_pi = jnp.exp(s_pi - logit_scale)
        exp_pi[g] = e_pi
        text_row = jnp.sum(e_pi[:H], axis=0, keepdims=True)
        audio_row = jnp.sum(e_pi[H:], axis=0, keepdims=True)
        line = lax.broadcasted_iota(jnp.int32, (8, M), 0)
        stat_c[c, g] = jnp.where(
            line == 0, text_row, jnp.where(line == 1, audio_row, diagonal)
        )
        e_ip = jnp.exp(logit_scale * contract(images, pairs, 1, 1) - logit_scale)
        exp_ip[g] = e_ip
        column = jnp.broadcast_to(jnp.sum(e_ip, axis=0, keepdims=True), (8, Q))
        if G == 1:
            stat_r[r] = column
        else:
            stat_r[r] = jnp.where(g == 0, column, stat_r[r] + column)

    if G > 1:
        stat_r[r] = jnp.zeros((8, Q), jnp.float32)
    loop(G, exps)
    for p in cols:
        go(to_col(stat_c.at[c], stat_c.at[c], sc_s, sc_r, p))
    for p in rows:
        go(to_row(stat_r.at[r], stat_r.at[r], sr_s, sr_r, p))
    for p in rows:
        from_row(stat_r.at[p], sr_s, sr_r, p)
    for p in cols:
        from_col(stat_c.at[p], sc_s, sc_r, p)

    columns = stat_r[0]
    for p in range(1, R):
        columns = columns + stat_r[p]
    columns = columns[0:1]
    inverse_c = 1.0 / columns
    inverse_c_tall = jnp.transpose(jnp.broadcast_to(inverse_c, (128, Q)))
    inverse_c_tall = jnp.concatenate([inverse_c_tall] * (M // 128), axis=1)
    loss_c[c] = jnp.broadcast_to(jnp.sum(jnp.log(columns), keepdims=True), (8, 128))

    def weights(g):
        totals = stat_c[0, g]
        for p in range(1, C):
            totals = totals + stat_c[p, g]
        text_row, audio_row, diagonal = totals[0:1], totals[1:2], totals[2:3]
        loss_part = jnp.sum(
            jnp.log(text_row) + jnp.log(audio_row) - 2.0 * diagonal, keepdims=True
        )
        loss_part = jnp.broadcast_to(loss_part, (8, 128))
        if G == 1:
            loss_r[r] = loss_part
        else:
            loss_r[r] = loss_r[r] + loss_part
        inverse_text = jnp.broadcast_to(1.0 / text_row, (H, M))
        inverse_audio = jnp.broadcast_to(1.0 / audio_row, (H, M))
        w_pi = exp_pi[g] * (
            jnp.concatenate([inverse_text, inverse_audio], axis=0) + inverse_c_tall
        )
        same_pi = block_ids(B, (1, M), 1, R, r + g * (B * R)) == block_ids(R, (Q, 1), 0, C, c)
        w_pi = (w_pi - jnp.where(same_pi, 2.0, 0.0)).astype(jnp.bfloat16)
        w_ip = exp_ip[g] * (
            jnp.concatenate([jnp.transpose(inverse_text), jnp.transpose(inverse_audio)], axis=1)
            + inverse_c
        )
        same_ip = block_ids(B, (M, 1), 0, R, r + g * (B * R)) == block_ids(R, (1, Q), 1, C, c)
        w_ip = (w_ip - jnp.where(same_ip, 2.0, 0.0)).astype(jnp.bfloat16)
        pairs = pair[...].reshape(Q, F)
        part_i[pl.ds(g * B, B)] = (
            contract(w_ip, pairs, 1, 0).astype(jnp.bfloat16).reshape(B, n, F)
        )
        images = img[pl.ds(g * B, B)].reshape(M, F)
        product = contract(w_pi, images, 1, 0)
        if G == 1:
            part_p[...] = product.astype(jnp.bfloat16).reshape(2, R, n, F)
        else:
            acc[...] = acc[...] + product

    if G > 1:
        loss_r[r] = jnp.zeros((8, 128), jnp.float32)
        acc[...] = jnp.zeros_like(acc)
    loop(G, weights)
    if G > 1:
        part_p[...] = acc[...].astype(jnp.bfloat16).reshape(2, R, n, F)

    for p in cols:
        go(to_col(part_i.at[p], recv_i.at[c], pi_s, pi_r, p))
    for p in rows:
        go(to_row(part_p.at[:, p], recv_p.at[:, r], pp_s, pp_r, p))
    for p in cols:
        go(to_col(loss_c.at[c], loss_c.at[c], lc_s, lc_r, p))
    for p in rows:
        go(to_row(loss_r.at[r], loss_r.at[r], lr_s, lr_r, p))

    def finish(values_ref, out_ref, gradient):
        values = values_ref[...].astype(jnp.float32)
        inverse = inverse_radius(values)
        unit = values * inverse
        gradient = logit_scale * gradient
        inner = jnp.sum(unit * gradient, axis=-1, keepdims=True)
        out_ref[...] = (gradient - unit * inner) * inverse

    text_sum = part_p[0, r].astype(jnp.float32)
    audio_sum = part_p[1, r].astype(jnp.float32)
    for p in rows:
        from_row(recv_p.at[:, p], pp_s, pp_r, p)
        text_sum = text_sum + recv_p[0, p].astype(jnp.float32)
        audio_sum = audio_sum + recv_p[1, p].astype(jnp.float32)
    finish(text_ref, text_out, text_sum)
    finish(audio_ref, audio_out, audio_sum)
    image_sum = part_i[c].astype(jnp.float32)
    for p in cols:
        from_col(recv_i.at[p], pi_s, pi_r, p)
        image_sum = image_sum + recv_i[p].astype(jnp.float32)
    finish(image_ref, image_out, image_sum)
    for p in cols:
        from_col(loss_c.at[p], lc_s, lc_r, p)
    for p in rows:
        from_row(loss_r.at[p], lr_s, lr_r, p)
    total = loss_c[0]
    for p in range(1, C):
        total = total + loss_c[p]
    for p in range(R):
        total = total + loss_r[p]
    loss_out[0, 0] = jnp.max(total) / (4.0 * n * R * C) + logit_scale
    for copy in sent:
        copy.wait_send()


def solution(mesh):
    R, C = mesh.shape["row"], mesh.shape["col"]

    def shards(image, text, audio):
        n, F = image.shape
        G = max(1, C // 8)
        B = C // G
        M, Q = B * n, 2 * R * n
        vmem = pl.BlockSpec(memory_space=pltpu.VMEM)
        f32, bf16 = jnp.float32, jnp.bfloat16
        grad = jax.ShapeDtypeStruct((n, F), f32)
        sem = pltpu.SemaphoreType.DMA
        sems = []
        for count in (C, R, C, R, C, R, C, R):
            sems += [sem((count,)), sem((count,))]
        image_grad, text_grad, audio_grad, loss = pl.pallas_call(
            functools.partial(kernel, R, C, n, F, G),
            out_shape=(grad, grad, grad, jax.ShapeDtypeStruct((1, 1), f32)),
            in_specs=[vmem] * 3,
            out_specs=(vmem, vmem, vmem, pl.BlockSpec(memory_space=pltpu.SMEM)),
            scratch_shapes=[
                pltpu.VMEM((C, n, F), bf16),
                pltpu.VMEM((2, R, n, F), bf16),
                pltpu.VMEM((G, M, Q), f32),
                pltpu.VMEM((G, Q, M), f32),
                pltpu.VMEM((C, G, 8, M), f32),
                pltpu.VMEM((R, 8, Q), f32),
                pltpu.VMEM((C, 8, 128), f32),
                pltpu.VMEM((R, 8, 128), f32),
                pltpu.VMEM((C, n, F), bf16),
                pltpu.VMEM((C, n, F), bf16),
                pltpu.VMEM((2, R, n, F), bf16),
                pltpu.VMEM((2, R, n, F), bf16),
                pltpu.VMEM((Q, F) if G > 1 else (8, 128), f32),
            ]
            + sems,
            compiler_params=pltpu.CompilerParams(collective_id=0, has_side_effects=True),
        )(image, text, audio)
        return image_grad, text_grad, audio_grad, loss.reshape(())

    first, second = P(("col", "row"), None), P(("row", "col"), None)
    return jax.shard_map(
        shards,
        mesh=mesh,
        in_specs=(first, second, second),
        out_specs=(first, second, second, P()),
        check_vma=False,
    )
```

```python
import functools

import jax
import jax.numpy as jnp
from jax import lax
from jax.experimental import pallas as pl
from jax.experimental.pallas import tpu as pltpu
from jax.sharding import PartitionSpec as P

MESH = pl.DeviceIdType.MESH
logit_scale = 20.0
epsilon = 1e-06


def inverse_radius(values):
    return lax.rsqrt(jnp.sum(values * values, axis=-1, keepdims=True) + epsilon)


def contract(left, right, left_dim, right_dim):
    return lax.dot_general(
        left, right, (((left_dim,), (right_dim,)), ((), ())), preferred_element_type=jnp.float32
    )


def kernel(
    R, C, X, n, F,
    image_ref, text_ref, audio_ref,
    image_out, text_out, audio_out, loss_out,
    img, pair, stat_a, stat_b, loss_a, loss_b,
    part_i, recv_i, acc, part_p, recv_h, recv_p,
    img_s, img_r, sa_s, sa_r, la_s, la_r, pi_s, pi_r,
    pair_s, pair_r, sb_s, sb_r, lb_s, lb_r, ph_s, ph_r, pp_s, pp_r, fw_s,
):
    r = lax.axis_index("row")
    c = lax.axis_index("col")
    A, B = C // X, R * X
    M, H = A * n, B * n
    Q = 2 * H
    a = lax.div(c, X)
    x = lax.rem(c, X)
    b = r * X + x
    step = 2 if R % 2 == 0 else 1
    sibling = r + 1 - 2 * lax.rem(r, 2)
    lines = [lax.rem(a + k, A) for k in range(1, A)]
    planes = [lax.rem(b + k, B) for k in range(1, B)]
    turns = [
        (lax.rem(r + i, R), lax.rem(x + j, X))
        for i in range(R - step, -1, -step)
        for j in range(X - 1, -1, -1)
    ]
    mates = [p * X + q for p, q in turns[:-1]]
    crossed = [(p + sibling - r) * X + q for p, q in turns] if step == 2 else []

    def line(p):
        return (r, p * X + x)

    def plane(p):
        return (lax.div(p, X), a * X + lax.rem(p, X))

    def copy(src, dst, send, recv, device):
        return pltpu.make_async_remote_copy(
            src_ref=src, dst_ref=dst, send_sem=send, recv_sem=recv,
            device_id=device, device_id_type=MESH,
        )

    sent = []

    def go(*args):
        one = copy(*args)
        one.start()
        sent.append(one)

    def arrive(dst, send, recv, device):
        copy(dst, dst, send, recv, device).wait_recv()

    barrier = pltpu.get_barrier_semaphore()
    for p in lines[::-1]:
        pl.semaphore_signal(barrier, inc=1, device_id=line(p), device_id_type=MESH)
    for p in planes:
        pl.semaphore_signal(barrier, inc=1, device_id=plane(p), device_id_type=MESH)

    v = image_ref[...].astype(jnp.float32)
    img[a] = (v * inverse_radius(v)).astype(jnp.bfloat16)
    v = text_ref[...].astype(jnp.float32)
    pair[0, b] = (v * inverse_radius(v)).astype(jnp.bfloat16)
    v = audio_ref[...].astype(jnp.float32)
    pair[1, b] = (v * inverse_radius(v)).astype(jnp.bfloat16)

    pl.semaphore_wait(barrier, A - 1 + B - 1)
    for p in mates:
        go(pair.at[:, b], pair.at[:, b], pair_s.at[p], pair_r.at[b], plane(p))
    for p in lines:
        go(img.at[a], img.at[a], img_s.at[p], img_r.at[a], line(p))
    if step == 2:
        go(pair.at[:, b], pair.at[:, b], fw_s.at[b], pair_r.at[b], (sibling, c))
    for p in mates[::-1]:
        arrive(pair.at[:, p], pair_s.at[p], pair_r.at[p], plane(p))
        if step == 2:
            go(pair.at[:, p], pair.at[:, p], fw_s.at[p], pair_r.at[p], (sibling, c))
    for p in lines:
        arrive(img.at[p], img_s.at[p], img_r.at[p], line(p))
    for p in crossed:
        arrive(pair.at[:, p], fw_s.at[p], pair_r.at[p], (sibling, c))

    def image_ids(shape, axis):
        local = lax.broadcasted_iota(jnp.int32, shape, axis)
        return ((lax.div(local, n) * X + x) * R + r) * n + lax.rem(local, n)

    def pair_ids(shape, axis):
        local = lax.rem(lax.broadcasted_iota(jnp.int32, shape, axis), H)
        block = lax.div(local, n)
        block = lax.div(block, X) * C + a * X + lax.rem(block, X)
        return block * n + lax.rem(local, n)

    images = img[...].reshape(M, F)
    pairs = pair[...].reshape(Q, F)
    s_pi = logit_scale * contract(pairs, images, 1, 1)
    same_pi = image_ids((1, M), 1) == pair_ids((Q, 1), 0)
    diagonal = jnp.sum(jnp.where(same_pi, s_pi, 0.0), axis=0, keepdims=True)
    e_pi = jnp.exp(s_pi - logit_scale)
    text_row = jnp.sum(e_pi[:H], axis=0, keepdims=True)
    audio_row = jnp.sum(e_pi[H:], axis=0, keepdims=True)
    index = lax.broadcasted_iota(jnp.int32, (8, M), 0)
    stat_a[a] = jnp.where(index == 0, text_row, jnp.where(index == 1, audio_row, diagonal))
    for p in lines:
        go(stat_a.at[a], stat_a.at[a], sa_s.at[p], sa_r.at[a], line(p))
    e_ip = jnp.exp(logit_scale * contract(images, pairs, 1, 1) - logit_scale)
    column = jnp.sum(e_ip, axis=0, keepdims=True)
    pieces = [column[:, k : k + 128] for k in range(0, Q, 128)]
    pieces = pieces * max(1, 8 // len(pieces))
    stat_b[b] = jnp.concatenate(pieces, axis=0)
    for p in planes:
        go(stat_b.at[b], stat_b.at[b], sb_s.at[p], sb_r.at[b], plane(p))
    for p in planes:
        arrive(stat_b.at[p], sb_s.at[p], sb_r.at[p], plane(p))
    columns = stat_b[0]
    for p in range(1, B):
        columns = columns + stat_b[p]
    columns = jnp.concatenate([columns[k : k + 1] for k in range(Q // 128)], axis=1)
    inverse_c = 1.0 / columns
    inverse_c_tall = jnp.transpose(jnp.broadcast_to(inverse_c, (128, Q)))
    inverse_c_tall = jnp.concatenate([inverse_c_tall] * (M // 128), axis=1)
    loss_a[a] = jnp.broadcast_to(jnp.sum(jnp.log(columns), keepdims=True), (8, 128))

    for p in lines:
        arrive(stat_a.at[p], sa_s.at[p], sa_r.at[p], line(p))
    totals = stat_a[0]
    for p in range(1, A):
        totals = totals + stat_a[p]
    text_row, audio_row, diagonal = totals[0:1], totals[1:2], totals[2:3]
    loss_part = jnp.sum(jnp.log(text_row) + jnp.log(audio_row) - 2.0 * diagonal, keepdims=True)
    loss_b[b] = jnp.broadcast_to(loss_part, (8, 128))
    inverse_text = jnp.broadcast_to(1.0 / text_row, (H, M))
    inverse_audio = jnp.broadcast_to(1.0 / audio_row, (H, M))
    w_pi = e_pi * (jnp.concatenate([inverse_text, inverse_audio], axis=0) + inverse_c_tall)
    w_pi = (w_pi - jnp.where(same_pi, 2.0, 0.0)).astype(jnp.bfloat16)
    acc[...] = contract(w_pi, images, 1, 0).reshape(2, B, n, F)
    for p in crossed:
        part_p[:, p] = acc[:, p].astype(jnp.bfloat16)
        go(part_p.at[:, p], recv_h.at[:, p], ph_s.at[p], ph_r.at[p], (sibling, c))

    same_ip = image_ids((M, 1), 0) == pair_ids((1, Q), 1)
    inverse_rows = jnp.concatenate(
        [jnp.transpose(inverse_text), jnp.transpose(inverse_audio)], axis=1
    )
    w_ip = e_ip * (inverse_rows + inverse_c)
    w_ip = (w_ip - jnp.where(same_ip, 2.0, 0.0)).astype(jnp.bfloat16)
    part_i[...] = contract(w_ip, pairs, 1, 0).astype(jnp.bfloat16).reshape(A, n, F)
    for p in lines:
        go(part_i.at[p], recv_i.at[a], pi_s.at[p], pi_r.at[a], line(p))
    for p in mates:
        if step == 2:
            arrive(recv_h.at[:, p], ph_s.at[p], ph_r.at[p], (sibling, c))
            part_p[:, p] = (acc[:, p] + recv_h[:, p].astype(jnp.float32)).astype(jnp.bfloat16)
        else:
            part_p[:, p] = acc[:, p].astype(jnp.bfloat16)
        go(part_p.at[:, p], recv_p.at[:, b], pp_s.at[p], pp_r.at[b], plane(p))
    for p in lines:
        go(loss_a.at[a], loss_a.at[a], la_s.at[p], la_r.at[a], line(p))
    for p in planes:
        go(loss_b.at[b], loss_b.at[b], lb_s.at[p], lb_r.at[b], plane(p))

    def finish(values_ref, out_ref, gradient):
        values = values_ref[...].astype(jnp.float32)
        inverse = inverse_radius(values)
        unit = values * inverse
        gradient = logit_scale * gradient
        inner = jnp.sum(unit * gradient, axis=-1, keepdims=True)
        out_ref[...] = (gradient - unit * inner) * inverse

    pair_sum = acc[:, b]
    if step == 2:
        arrive(recv_h.at[:, b], ph_s.at[b], ph_r.at[b], (sibling, c))
        pair_sum = pair_sum + recv_h[:, b].astype(jnp.float32)
    for p in mates[::-1]:
        arrive(recv_p.at[:, p], pp_s.at[p], pp_r.at[p], plane(p))
        pair_sum = pair_sum + recv_p[:, p].astype(jnp.float32)
    finish(text_ref, text_out, pair_sum[0])
    finish(audio_ref, audio_out, pair_sum[1])
    image_sum = part_i[a].astype(jnp.float32)
    for p in lines:
        arrive(recv_i.at[p], pi_s.at[p], pi_r.at[p], line(p))
        image_sum = image_sum + recv_i[p].astype(jnp.float32)
    finish(image_ref, image_out, image_sum)
    for p in lines:
        arrive(loss_a.at[p], la_s.at[p], la_r.at[p], line(p))
    for p in planes:
        arrive(loss_b.at[p], lb_s.at[p], lb_r.at[p], plane(p))
    total = loss_a[0]
    for p in range(1, A):
        total = total + loss_a[p]
    for p in range(B):
        total = total + loss_b[p]
    loss_out[0, 0] = jnp.max(total) / (4.0 * n * R * C) + logit_scale
    for one in sent:
        one.wait_send()


def solution(mesh):
    R, C = mesh.shape["row"], mesh.shape["col"]
    X = 1
    while R * X < C // X and C % (2 * X) == 0:
        X *= 2
    A, B = C // X, R * X

    def shards(image, text, audio):
        n, F = image.shape
        M, Q = A * n, 2 * B * n
        vmem = pl.BlockSpec(memory_space=pltpu.VMEM)
        f32, bf16 = jnp.float32, jnp.bfloat16
        grad = pltpu.VMEM((n, F), f32)
        sem = pltpu.SemaphoreType.DMA
        sems = [sem((A,))] * 8 + [sem((B,))] * 11
        image_grad, text_grad, audio_grad, loss = pl.pallas_call(
            functools.partial(kernel, R, C, X, n, F),
            out_shape=(grad, grad, grad, jax.ShapeDtypeStruct((1, 1), f32)),
            in_specs=[vmem] * 3,
            out_specs=(vmem, vmem, vmem, pl.BlockSpec(memory_space=pltpu.SMEM)),
            scratch_shapes=[
                pltpu.VMEM((A, n, F), bf16),
                pltpu.VMEM((2, B, n, F), bf16),
                pltpu.VMEM((A, 8, M), f32),
                pltpu.VMEM((B, max(8, Q // 128), 128), f32),
                pltpu.VMEM((A, 8, 128), f32),
                pltpu.VMEM((B, 8, 128), f32),
                pltpu.VMEM((A, n, F), bf16),
                pltpu.VMEM((A, n, F), bf16),
                pltpu.VMEM((2, B, n, F), f32),
                pltpu.VMEM((2, B, n, F), bf16),
                pltpu.VMEM((2, B, n, F), bf16),
                pltpu.VMEM((2, B, n, F), bf16),
            ]
            + sems,
            compiler_params=pltpu.CompilerParams(
                collective_id=0, has_side_effects=True, vmem_limit_bytes=48 << 20
            ),
        )(image, text, audio)
        return image_grad, text_grad, audio_grad, loss.reshape(())

    first, second = P(("col", "row"), None), P(("row", "col"), None)
    return jax.shard_map(
        shards,
        mesh=mesh,
        in_specs=(first, second, second),
        out_specs=(first, second, second, P()),
        check_vma=False,
    )
```

```python
import functools

import jax
import jax.numpy as jnp
from jax import lax
from jax.experimental import pallas as pl
from jax.experimental.pallas import tpu as pltpu
from jax.sharding import PartitionSpec as P

MESH = pl.DeviceIdType.MESH
logit_scale = 20.0
epsilon = 1e-06


def inverse_radius(values):
    return lax.rsqrt(jnp.sum(values * values, axis=-1, keepdims=True) + epsilon)


def contract(left, right, left_dim, right_dim):
    return lax.dot_general(
        left, right, (((left_dim,), (right_dim,)), ((), ())), preferred_element_type=jnp.float32
    )


def kernel(
    R, C, X, n, F,
    image_hbm, text_hbm, audio_hbm,
    image_out, text_out, audio_out, loss_out,
    img, pair, stat_a, stat_b, loss_a, loss_b,
    part_i, recv_i, acc, part_p, recv_h, recv_p,
    img_s, img_r, sa_s, sa_r, la_s, la_r, pi_s, pi_r,
    pair_s, pair_r, sb_s, sb_r, lb_s, lb_r, ph_s, ph_r, pp_s, pp_r, fw_s,
    image_ref, text_ref, audio_ref, load_s,
):
    r = lax.axis_index("row")
    c = lax.axis_index("col")
    A, B = C // X, R * X
    M, H = A * n, B * n
    Q = 2 * H
    a = lax.div(c, X)
    x = lax.rem(c, X)
    b = r * X + x
    step = 2 if R % 2 == 0 else 1
    sibling = r + 1 - 2 * lax.rem(r, 2)
    lines = [lax.rem(a + k, A) for k in range(1, A)]
    planes = [lax.rem(b + k, B) for k in range(1, B)]
    turns = [
        (lax.rem(r + i, R), lax.rem(x + j, X))
        for i in range(R - step, -1, -step)
        for j in range(X - 1, -1, -1)
    ]
    mates = [p * X + q for p, q in turns[:-1]]
    crossed = [(p + sibling - r) * X + q for p, q in turns] if step == 2 else []

    def line(p):
        return (r, p * X + x)

    def plane(p):
        return (lax.div(p, X), a * X + lax.rem(p, X))

    def copy(src, dst, send, recv, device):
        return pltpu.make_async_remote_copy(
            src_ref=src, dst_ref=dst, send_sem=send, recv_sem=recv,
            device_id=device, device_id_type=MESH,
        )

    sent = []

    def go(*args):
        one = copy(*args)
        one.start()
        sent.append(one)

    def arrive(dst, send, recv, device):
        copy(dst, dst, send, recv, device).wait_recv()

    barrier = pltpu.get_barrier_semaphore()
    for p in lines[::-1]:
        pl.semaphore_signal(barrier, inc=1, device_id=line(p), device_id_type=MESH)
    for p in planes:
        pl.semaphore_signal(barrier, inc=1, device_id=plane(p), device_id_type=MESH)

    loads = [
        pltpu.make_async_copy(src, dst, load_s.at[k])
        for k, (src, dst) in enumerate(
            ((text_hbm, text_ref), (audio_hbm, audio_ref), (image_hbm, image_ref))
        )
    ]
    for load in loads:
        load.start()
    loads[0].wait()
    v = text_ref[...].astype(jnp.float32)
    pair[0, b] = (v * inverse_radius(v)).astype(jnp.bfloat16)
    loads[1].wait()
    v = audio_ref[...].astype(jnp.float32)
    pair[1, b] = (v * inverse_radius(v)).astype(jnp.bfloat16)
    loads[2].wait()
    v = image_ref[...].astype(jnp.float32)
    img[a] = (v * inverse_radius(v)).astype(jnp.bfloat16)

    pl.semaphore_wait(barrier, A - 1 + B - 1)
    for p in mates:
        go(pair.at[:, b], pair.at[:, b], pair_s.at[p], pair_r.at[b], plane(p))
    for p in lines:
        go(img.at[a], img.at[a], img_s.at[p], img_r.at[a], line(p))
    if step == 2:
        go(pair.at[:, b], pair.at[:, b], fw_s.at[b], pair_r.at[b], (sibling, c))
    for p in mates[::-1]:
        arrive(pair.at[:, p], pair_s.at[p], pair_r.at[p], plane(p))
        if step == 2:
            go(pair.at[:, p], pair.at[:, p], fw_s.at[p], pair_r.at[p], (sibling, c))
    for p in lines:
        arrive(img.at[p], img_s.at[p], img_r.at[p], line(p))
    for p in crossed:
        arrive(pair.at[:, p], fw_s.at[p], pair_r.at[p], (sibling, c))

    def image_ids(shape, axis):
        local = lax.broadcasted_iota(jnp.int32, shape, axis)
        return ((lax.div(local, n) * X + x) * R + r) * n + lax.rem(local, n)

    def pair_ids(shape, axis):
        local = lax.rem(lax.broadcasted_iota(jnp.int32, shape, axis), H)
        block = lax.div(local, n)
        block = lax.div(block, X) * C + a * X + lax.rem(block, X)
        return block * n + lax.rem(local, n)

    images = img[...].reshape(M, F)
    pairs = pair[...].reshape(Q, F)
    s_pi = logit_scale * contract(pairs, images, 1, 1)
    same_pi = image_ids((1, M), 1) == pair_ids((Q, 1), 0)
    diagonal = jnp.sum(jnp.where(same_pi, s_pi, 0.0), axis=0, keepdims=True)
    e_pi = jnp.exp(s_pi - logit_scale)
    text_row = jnp.sum(e_pi[:H], axis=0, keepdims=True)
    audio_row = jnp.sum(e_pi[H:], axis=0, keepdims=True)
    index = lax.broadcasted_iota(jnp.int32, (8, M), 0)
    stat_a[a] = jnp.where(index == 0, text_row, jnp.where(index == 1, audio_row, diagonal))
    for p in lines:
        go(stat_a.at[a], stat_a.at[a], sa_s.at[p], sa_r.at[a], line(p))
    e_ip = jnp.exp(logit_scale * contract(images, pairs, 1, 1) - logit_scale)
    column = jnp.sum(e_ip, axis=0, keepdims=True)
    pieces = [column[:, k : k + 128] for k in range(0, Q, 128)]
    pieces = pieces * max(1, 8 // len(pieces))
    stat_b[b] = jnp.concatenate(pieces, axis=0)
    for p in planes:
        go(stat_b.at[b], stat_b.at[b], sb_s.at[p], sb_r.at[b], plane(p))
    for p in planes:
        arrive(stat_b.at[p], sb_s.at[p], sb_r.at[p], plane(p))
    columns = stat_b[0]
    for p in range(1, B):
        columns = columns + stat_b[p]
    columns = jnp.concatenate([columns[k : k + 1] for k in range(Q // 128)], axis=1)
    inverse_c = 1.0 / columns
    inverse_c_tall = jnp.transpose(jnp.broadcast_to(inverse_c, (128, Q)))
    inverse_c_tall = jnp.concatenate([inverse_c_tall] * (M // 128), axis=1)
    loss_a[a] = jnp.broadcast_to(jnp.sum(jnp.log(columns), keepdims=True), (8, 128))

    for p in lines:
        arrive(stat_a.at[p], sa_s.at[p], sa_r.at[p], line(p))
    totals = stat_a[0]
    for p in range(1, A):
        totals = totals + stat_a[p]
    text_row, audio_row, diagonal = totals[0:1], totals[1:2], totals[2:3]
    loss_part = jnp.sum(jnp.log(text_row) + jnp.log(audio_row) - 2.0 * diagonal, keepdims=True)
    loss_b[b] = jnp.broadcast_to(loss_part, (8, 128))
    inverse_text = jnp.broadcast_to(1.0 / text_row, (H, M))
    inverse_audio = jnp.broadcast_to(1.0 / audio_row, (H, M))
    w_pi = e_pi * (jnp.concatenate([inverse_text, inverse_audio], axis=0) + inverse_c_tall)
    w_pi = (w_pi - jnp.where(same_pi, 2.0, 0.0)).astype(jnp.bfloat16)
    acc[...] = contract(w_pi, images, 1, 0).reshape(2, B, n, F)
    for p in crossed:
        part_p[:, p] = acc[:, p].astype(jnp.bfloat16)
        go(part_p.at[:, p], recv_h.at[:, p], ph_s.at[p], ph_r.at[p], (sibling, c))

    same_ip = image_ids((M, 1), 0) == pair_ids((1, Q), 1)
    inverse_rows = jnp.concatenate(
        [jnp.transpose(inverse_text), jnp.transpose(inverse_audio)], axis=1
    )
    w_ip = e_ip * (inverse_rows + inverse_c)
    w_ip = (w_ip - jnp.where(same_ip, 2.0, 0.0)).astype(jnp.bfloat16)
    part_i[...] = contract(w_ip, pairs, 1, 0).astype(jnp.bfloat16).reshape(A, n, F)
    for p in lines:
        go(part_i.at[p], recv_i.at[a], pi_s.at[p], pi_r.at[a], line(p))
    for p in mates:
        if step == 2:
            arrive(recv_h.at[:, p], ph_s.at[p], ph_r.at[p], (sibling, c))
            part_p[:, p] = (acc[:, p] + recv_h[:, p].astype(jnp.float32)).astype(jnp.bfloat16)
        else:
            part_p[:, p] = acc[:, p].astype(jnp.bfloat16)
        go(part_p.at[:, p], recv_p.at[:, b], pp_s.at[p], pp_r.at[b], plane(p))
    for p in lines:
        go(loss_a.at[a], loss_a.at[a], la_s.at[p], la_r.at[a], line(p))
    for p in planes:
        go(loss_b.at[b], loss_b.at[b], lb_s.at[p], lb_r.at[b], plane(p))

    def finish(values_ref, out_ref, gradient):
        values = values_ref[...].astype(jnp.float32)
        inverse = inverse_radius(values)
        unit = values * inverse
        gradient = logit_scale * gradient
        inner = jnp.sum(unit * gradient, axis=-1, keepdims=True)
        out_ref[...] = (gradient - unit * inner) * inverse

    pair_sum = acc[:, b]
    if step == 2:
        arrive(recv_h.at[:, b], ph_s.at[b], ph_r.at[b], (sibling, c))
        pair_sum = pair_sum + recv_h[:, b].astype(jnp.float32)
    for p in mates[::-1]:
        arrive(recv_p.at[:, p], pp_s.at[p], pp_r.at[p], plane(p))
        pair_sum = pair_sum + recv_p[:, p].astype(jnp.float32)
    finish(text_ref, text_out, pair_sum[0])
    finish(audio_ref, audio_out, pair_sum[1])
    image_sum = part_i[a].astype(jnp.float32)
    for p in lines:
        arrive(recv_i.at[p], pi_s.at[p], pi_r.at[p], line(p))
        image_sum = image_sum + recv_i[p].astype(jnp.float32)
    finish(image_ref, image_out, image_sum)
    for p in lines:
        arrive(loss_a.at[p], la_s.at[p], la_r.at[p], line(p))
    for p in planes:
        arrive(loss_b.at[p], lb_s.at[p], lb_r.at[p], plane(p))
    total = loss_a[0]
    for p in range(1, A):
        total = total + loss_a[p]
    for p in range(B):
        total = total + loss_b[p]
    loss_out[0, 0] = jnp.max(total) / (4.0 * n * R * C) + logit_scale
    for one in sent:
        one.wait_send()


def write_back(a_ref, b_ref, c_ref, a_out, b_out, c_out, done):
    copies = [
        pltpu.make_async_copy(src, dst, done.at[k])
        for k, (src, dst) in enumerate(((a_ref, a_out), (b_ref, b_out), (c_ref, c_out)))
    ]
    for copy in copies:
        copy.start()
    for copy in copies:
        copy.wait()


def solution(mesh):
    R, C = mesh.shape["row"], mesh.shape["col"]
    X = 1
    while R * X < C // X and C % (2 * X) == 0:
        X *= 2
    A, B = C // X, R * X

    def shards(image, text, audio):
        n, F = image.shape
        M, Q = A * n, 2 * B * n
        vmem = pl.BlockSpec(memory_space=pltpu.VMEM)
        hbm = pl.BlockSpec(memory_space=pltpu.HBM)
        f32, bf16 = jnp.float32, jnp.bfloat16
        grad = pltpu.VMEM((n, F), f32)
        sem = pltpu.SemaphoreType.DMA
        sems = [sem((A,))] * 8 + [sem((B,))] * 11
        image_grad, text_grad, audio_grad, loss = pl.pallas_call(
            functools.partial(kernel, R, C, X, n, F),
            out_shape=(grad, grad, grad, jax.ShapeDtypeStruct((1, 1), f32)),
            in_specs=[hbm] * 3,
            out_specs=(vmem, vmem, vmem, pl.BlockSpec(memory_space=pltpu.SMEM)),
            scratch_shapes=[
                pltpu.VMEM((A, n, F), bf16),
                pltpu.VMEM((2, B, n, F), bf16),
                pltpu.VMEM((A, 8, M), f32),
                pltpu.VMEM((B, max(8, Q // 128), 128), f32),
                pltpu.VMEM((A, 8, 128), f32),
                pltpu.VMEM((B, 8, 128), f32),
                pltpu.VMEM((A, n, F), bf16),
                pltpu.VMEM((A, n, F), bf16),
                pltpu.VMEM((2, B, n, F), f32),
                pltpu.VMEM((2, B, n, F), bf16),
                pltpu.VMEM((2, B, n, F), bf16),
                pltpu.VMEM((2, B, n, F), bf16),
            ]
            + sems
            + [pltpu.VMEM((n, F), bf16)] * 3
            + [sem((3,))],
            compiler_params=pltpu.CompilerParams(
                collective_id=0, has_side_effects=True, vmem_limit_bytes=67043328 - 13 * n * F
            ),
        )(image, text, audio)
        full = jax.ShapeDtypeStruct((n, F), f32)
        image_grad, text_grad, audio_grad = pl.pallas_call(
            write_back,
            out_shape=(full,) * 3,
            in_specs=[vmem] * 3,
            out_specs=(hbm,) * 3,
            scratch_shapes=[sem((3,))],
            compiler_params=pltpu.CompilerParams(vmem_limit_bytes=1 << 20),
        )(image_grad, text_grad, audio_grad)
        return image_grad, text_grad, audio_grad, loss.reshape(())

    first, second = P(("col", "row"), None), P(("row", "col"), None)
    return jax.shard_map(
        shards,
        mesh=mesh,
        in_specs=(first, second, second),
        out_specs=(first, second, second, P()),
        check_vma=False,
    )
```

```python
import functools

import jax
import jax.numpy as jnp
from jax import lax
from jax.experimental import pallas as pl
from jax.experimental.pallas import tpu as pltpu
from jax.sharding import PartitionSpec as P

MESH = pl.DeviceIdType.MESH
logit_scale = 20.0
epsilon = 1e-06


def inverse_radius(values):
    return lax.rsqrt(jnp.sum(values * values, axis=-1, keepdims=True) + epsilon)


def contract(left, right, left_dim, right_dim):
    return lax.dot_general(
        left, right, (((left_dim,), (right_dim,)), ((), ())), preferred_element_type=jnp.float32
    )


def kernel(
    R, C, X, n, F,
    image_hbm, text_hbm, audio_hbm,
    image_out, text_out, audio_out, loss_out,
    img, pair, stat_a, stat_b, loss_a, loss_b,
    part_i, recv_i, acc, part_p, recv_h, recv_p,
    img_s, img_r, sa_s, sa_r, la_s, la_r, pi_s, pi_r,
    pair_s, pair_r, sb_s, sb_r, lb_s, lb_r, ph_s, ph_r, pp_s, pp_r, fw_s,
    image_ref, text_ref, audio_ref, load_s,
):
    r = lax.axis_index("row")
    c = lax.axis_index("col")
    A, B = C // X, R * X
    M, H = A * n, B * n
    Q = 2 * H
    a = lax.div(c, X)
    x = lax.rem(c, X)
    b = r * X + x
    step = 2 if R % 2 == 0 else 1
    sibling = r + 1 - 2 * lax.rem(r, 2)
    side = 2 * lax.rem(a, 2) - 1
    far_first = sorted(range(1, A), key=lambda k: abs(2 * k - A))
    lines = [lax.rem(a + side * k + A, A) for k in far_first]
    planes = [lax.rem(b + k, B) for k in range(1, B)]
    turns = [
        (lax.rem(r + i, R), lax.rem(x + j, X))
        for i in range(R - step, -1, -step)
        for j in range(X - 1, -1, -1)
    ]
    mates = [p * X + q for p, q in turns[:-1]]
    crossed = [(p + sibling - r) * X + q for p, q in turns] if step == 2 else []

    def line(p):
        return (r, p * X + x)

    def plane(p):
        return (lax.div(p, X), a * X + lax.rem(p, X))

    def copy(src, dst, send, recv, device):
        return pltpu.make_async_remote_copy(
            src_ref=src, dst_ref=dst, send_sem=send, recv_sem=recv,
            device_id=device, device_id_type=MESH,
        )

    sent = []

    def go(*args):
        one = copy(*args)
        one.start()
        sent.append(one)

    def arrive(dst, send, recv, device):
        copy(dst, dst, send, recv, device).wait_recv()

    barrier = pltpu.get_barrier_semaphore()
    for p in lines[::-1]:
        pl.semaphore_signal(barrier, inc=1, device_id=line(p), device_id_type=MESH)
    for p in planes:
        pl.semaphore_signal(barrier, inc=1, device_id=plane(p), device_id_type=MESH)

    loads = [
        pltpu.make_async_copy(src, dst, load_s.at[k])
        for k, (src, dst) in enumerate(
            ((text_hbm, text_ref), (audio_hbm, audio_ref), (image_hbm, image_ref))
        )
    ]
    for load in loads:
        load.start()
    loads[0].wait()
    v = text_ref[...].astype(jnp.float32)
    pair[0, b] = (v * inverse_radius(v)).astype(jnp.bfloat16)
    loads[1].wait()
    v = audio_ref[...].astype(jnp.float32)
    pair[1, b] = (v * inverse_radius(v)).astype(jnp.bfloat16)
    loads[2].wait()
    v = image_ref[...].astype(jnp.float32)
    img[a] = (v * inverse_radius(v)).astype(jnp.bfloat16)

    pl.semaphore_wait(barrier, A - 1 + B - 1)
    for p in mates:
        go(pair.at[:, b], pair.at[:, b], pair_s.at[p], pair_r.at[b], plane(p))
    for p in lines:
        go(img.at[a], img.at[a], img_s.at[p], img_r.at[a], line(p))
    if step == 2:
        go(pair.at[:, b], pair.at[:, b], fw_s.at[b], pair_r.at[b], (sibling, c))
    for p in mates[::-1]:
        arrive(pair.at[:, p], pair_s.at[p], pair_r.at[p], plane(p))
        if step == 2:
            go(pair.at[:, p], pair.at[:, p], fw_s.at[p], pair_r.at[p], (sibling, c))
    for p in lines:
        arrive(img.at[p], img_s.at[p], img_r.at[p], line(p))
    for p in crossed:
        arrive(pair.at[:, p], fw_s.at[p], pair_r.at[p], (sibling, c))

    def image_ids(shape, axis):
        local = lax.broadcasted_iota(jnp.int32, shape, axis)
        return ((lax.div(local, n) * X + x) * R + r) * n + lax.rem(local, n)

    def pair_ids(shape, axis):
        local = lax.rem(lax.broadcasted_iota(jnp.int32, shape, axis), H)
        block = lax.div(local, n)
        block = lax.div(block, X) * C + a * X + lax.rem(block, X)
        return block * n + lax.rem(local, n)

    images = img[...].reshape(M, F)
    pairs = pair[...].reshape(Q, F)
    s_pi = logit_scale * contract(pairs, images, 1, 1)
    same_pi = image_ids((1, M), 1) == pair_ids((Q, 1), 0)
    diagonal = jnp.sum(jnp.where(same_pi, s_pi, 0.0), axis=0, keepdims=True)
    e_pi = jnp.exp(s_pi - logit_scale)
    text_row = jnp.sum(e_pi[:H], axis=0, keepdims=True)
    audio_row = jnp.sum(e_pi[H:], axis=0, keepdims=True)
    index = lax.broadcasted_iota(jnp.int32, (8, M), 0)
    stat_a[a] = jnp.where(index == 0, text_row, jnp.where(index == 1, audio_row, diagonal))
    for p in lines:
        go(stat_a.at[a], stat_a.at[a], sa_s.at[p], sa_r.at[a], line(p))
    e_ip = jnp.exp(logit_scale * contract(images, pairs, 1, 1) - logit_scale)
    column = jnp.sum(e_ip, axis=0, keepdims=True)
    pieces = [column[:, k : k + 128] for k in range(0, Q, 128)]
    pieces = pieces * max(1, 8 // len(pieces))
    stat_b[b] = jnp.concatenate(pieces, axis=0)
    for p in planes:
        go(stat_b.at[b], stat_b.at[b], sb_s.at[p], sb_r.at[b], plane(p))
    for p in planes:
        arrive(stat_b.at[p], sb_s.at[p], sb_r.at[p], plane(p))
    columns = stat_b[0]
    for p in range(1, B):
        columns = columns + stat_b[p]
    columns = jnp.concatenate([columns[k : k + 1] for k in range(Q // 128)], axis=1)
    inverse_c = 1.0 / columns
    inverse_c_tall = jnp.transpose(jnp.broadcast_to(inverse_c, (128, Q)))
    inverse_c_tall = jnp.concatenate([inverse_c_tall] * (M // 128), axis=1)
    loss_a[a] = jnp.broadcast_to(jnp.sum(jnp.log(columns), keepdims=True), (8, 128))
    for p in lines:
        go(loss_a.at[a], loss_a.at[a], la_s.at[p], la_r.at[a], line(p))

    for p in lines:
        arrive(stat_a.at[p], sa_s.at[p], sa_r.at[p], line(p))
    totals = stat_a[0]
    for p in range(1, A):
        totals = totals + stat_a[p]
    text_row, audio_row, diagonal = totals[0:1], totals[1:2], totals[2:3]
    loss_part = jnp.sum(jnp.log(text_row) + jnp.log(audio_row) - 2.0 * diagonal, keepdims=True)
    loss_b[b] = jnp.broadcast_to(loss_part, (8, 128))
    for p in planes:
        go(loss_b.at[b], loss_b.at[b], lb_s.at[p], lb_r.at[b], plane(p))
    inverse_text = jnp.broadcast_to(1.0 / text_row, (H, M))
    inverse_audio = jnp.broadcast_to(1.0 / audio_row, (H, M))
    w_pi = e_pi * (jnp.concatenate([inverse_text, inverse_audio], axis=0) + inverse_c_tall)
    w_pi = (w_pi - jnp.where(same_pi, 2.0, 0.0)).astype(jnp.bfloat16)
    acc[...] = contract(w_pi, images, 1, 0).reshape(2, B, n, F)
    for p in crossed:
        part_p[:, p] = acc[:, p].astype(jnp.bfloat16)
        go(part_p.at[:, p], recv_h.at[:, p], ph_s.at[p], ph_r.at[p], (sibling, c))

    same_ip = image_ids((M, 1), 0) == pair_ids((1, Q), 1)
    inverse_rows = jnp.concatenate(
        [jnp.transpose(inverse_text), jnp.transpose(inverse_audio)], axis=1
    )
    w_ip = e_ip * (inverse_rows + inverse_c)
    w_ip = (w_ip - jnp.where(same_ip, 2.0, 0.0)).astype(jnp.bfloat16)
    part_i[...] = contract(w_ip, pairs, 1, 0).astype(jnp.bfloat16).reshape(A, n, F)
    for p in lines:
        go(part_i.at[p], recv_i.at[a], pi_s.at[p], pi_r.at[a], line(p))
    for p in mates:
        if step == 2:
            arrive(recv_h.at[:, p], ph_s.at[p], ph_r.at[p], (sibling, c))
            part_p[:, p] = (acc[:, p] + recv_h[:, p].astype(jnp.float32)).astype(jnp.bfloat16)
        else:
            part_p[:, p] = acc[:, p].astype(jnp.bfloat16)
        go(part_p.at[:, p], recv_p.at[:, b], pp_s.at[p], pp_r.at[b], plane(p))

    def finish(values_ref, out_ref, gradient):
        values = values_ref[...].astype(jnp.float32)
        inverse = inverse_radius(values)
        unit = values * inverse
        gradient = logit_scale * gradient
        inner = jnp.sum(unit * gradient, axis=-1, keepdims=True)
        out_ref[...] = (gradient - unit * inner) * inverse

    pair_sum = acc[:, b]
    if step == 2:
        arrive(recv_h.at[:, b], ph_s.at[b], ph_r.at[b], (sibling, c))
        pair_sum = pair_sum + recv_h[:, b].astype(jnp.float32)
    for p in mates[::-1]:
        arrive(recv_p.at[:, p], pp_s.at[p], pp_r.at[p], plane(p))
        pair_sum = pair_sum + recv_p[:, p].astype(jnp.float32)
    finish(text_ref, text_out, pair_sum[0])
    finish(audio_ref, audio_out, pair_sum[1])
    image_sum = part_i[a].astype(jnp.float32)
    for p in lines:
        arrive(recv_i.at[p], pi_s.at[p], pi_r.at[p], line(p))
        image_sum = image_sum + recv_i[p].astype(jnp.float32)
    finish(image_ref, image_out, image_sum)
    for p in lines:
        arrive(loss_a.at[p], la_s.at[p], la_r.at[p], line(p))
    for p in planes:
        arrive(loss_b.at[p], lb_s.at[p], lb_r.at[p], plane(p))
    total = loss_a[0]
    for p in range(1, A):
        total = total + loss_a[p]
    for p in range(B):
        total = total + loss_b[p]
    loss_out[0, 0] = jnp.max(total) / (4.0 * n * R * C) + logit_scale
    for one in sent:
        one.wait_send()


def write_back(a_ref, b_ref, c_ref, a_out, b_out, c_out, done):
    copies = [
        pltpu.make_async_copy(src, dst, done.at[k])
        for k, (src, dst) in enumerate(((a_ref, a_out), (b_ref, b_out), (c_ref, c_out)))
    ]
    for copy in copies:
        copy.start()
    for copy in copies:
        copy.wait()


def solution(mesh):
    R, C = mesh.shape["row"], mesh.shape["col"]
    X = 1
    while R * X < C // X and C % (2 * X) == 0:
        X *= 2
    A, B = C // X, R * X

    def shards(image, text, audio):
        n, F = image.shape
        M, Q = A * n, 2 * B * n
        vmem = pl.BlockSpec(memory_space=pltpu.VMEM)
        hbm = pl.BlockSpec(memory_space=pltpu.HBM)
        f32, bf16 = jnp.float32, jnp.bfloat16
        grad = pltpu.VMEM((n, F), f32)
        sem = pltpu.SemaphoreType.DMA
        sems = [sem((A,))] * 8 + [sem((B,))] * 11
        image_grad, text_grad, audio_grad, loss = pl.pallas_call(
            functools.partial(kernel, R, C, X, n, F),
            out_shape=(grad, grad, grad, jax.ShapeDtypeStruct((1, 1), f32)),
            in_specs=[hbm] * 3,
            out_specs=(vmem, vmem, vmem, pl.BlockSpec(memory_space=pltpu.SMEM)),
            scratch_shapes=[
                pltpu.VMEM((A, n, F), bf16),
                pltpu.VMEM((2, B, n, F), bf16),
                pltpu.VMEM((A, 8, M), f32),
                pltpu.VMEM((B, max(8, Q // 128), 128), f32),
                pltpu.VMEM((A, 8, 128), f32),
                pltpu.VMEM((B, 8, 128), f32),
                pltpu.VMEM((A, n, F), bf16),
                pltpu.VMEM((A, n, F), bf16),
                pltpu.VMEM((2, B, n, F), f32),
                pltpu.VMEM((2, B, n, F), bf16),
                pltpu.VMEM((2, B, n, F), bf16),
                pltpu.VMEM((2, B, n, F), bf16),
            ]
            + sems
            + [pltpu.VMEM((n, F), bf16)] * 3
            + [sem((3,))],
            compiler_params=pltpu.CompilerParams(
                collective_id=0, has_side_effects=True, vmem_limit_bytes=67043328 - 13 * n * F
            ),
        )(image, text, audio)
        full = jax.ShapeDtypeStruct((n, F), f32)
        image_grad, text_grad, audio_grad = pl.pallas_call(
            write_back,
            out_shape=(full,) * 3,
            in_specs=[vmem] * 3,
            out_specs=(hbm,) * 3,
            scratch_shapes=[sem((3,))],
            compiler_params=pltpu.CompilerParams(vmem_limit_bytes=1 << 20),
        )(image_grad, text_grad, audio_grad)
        return image_grad, text_grad, audio_grad, loss.reshape(())

    first, second = P(("col", "row"), None), P(("row", "col"), None)
    return jax.shard_map(
        shards,
        mesh=mesh,
        in_specs=(first, second, second),
        out_specs=(first, second, second, P()),
        check_vma=False,
    )
```

```python
import functools

import jax
import jax.numpy as jnp
from jax import lax
from jax.experimental import pallas as pl
from jax.experimental.pallas import tpu as pltpu
from jax.sharding import PartitionSpec as P

MESH = pl.DeviceIdType.MESH
logit_scale = 20.0
epsilon = 1e-06


def inverse_radius(values):
    return lax.rsqrt(jnp.sum(values * values, axis=-1, keepdims=True) + epsilon)


def contract(left, right, left_dim, right_dim):
    return lax.dot_general(
        left, right, (((left_dim,), (right_dim,)), ((), ())), preferred_element_type=jnp.float32
    )


def kernel(
    R, C, X, n, F,
    image_hbm, text_hbm, audio_hbm,
    image_out, text_out, audio_out, loss_out,
    img, pair, stat_a, stat_b, loss_a, loss_b,
    part_i, recv_i, acc, part_p, recv_h, recv_p,
    img_s, img_r, sa_s, sa_r, la_s, la_r, pi_s, pi_r,
    pair_s, pair_r, sb_s, sb_r, lb_s, lb_r, ph_s, ph_r, pp_s, pp_r, fw_s,
    image_ref, text_ref, audio_ref, load_s,
):
    r = lax.axis_index("row")
    c = lax.axis_index("col")
    A, B = C // X, R * X
    M, H = A * n, B * n
    Q = 2 * H
    a = lax.div(c, X)
    x = lax.rem(c, X)
    b = r * X + x
    step = 2 if R % 2 == 0 else 1
    sibling = r + 1 - 2 * lax.rem(r, 2)
    side = 2 * lax.rem(a, 2) - 1
    far_first = sorted(range(1, A), key=lambda k: abs(2 * k - A))
    lines = [lax.rem(a + side * k + A, A) for k in far_first]
    planes = [lax.rem(b + k, B) for k in range(1, B)]
    turns = [
        (lax.rem(r + i, R), lax.rem(x + j, X))
        for i in range(R - step, -1, -step)
        for j in range(X - 1, -1, -1)
    ]
    mates = [p * X + q for p, q in turns[:-1]]
    crossed = [(p + sibling - r) * X + q for p, q in turns] if step == 2 else []

    def line(p):
        return (r, p * X + x)

    def plane(p):
        return (lax.div(p, X), a * X + lax.rem(p, X))

    def copy(src, dst, send, recv, device):
        return pltpu.make_async_remote_copy(
            src_ref=src, dst_ref=dst, send_sem=send, recv_sem=recv,
            device_id=device, device_id_type=MESH,
        )

    sent = []

    def go(*args):
        one = copy(*args)
        one.start()
        sent.append(one)

    def arrive(dst, send, recv, device):
        copy(dst, dst, send, recv, device).wait_recv()

    barrier = pltpu.get_barrier_semaphore()
    for p in lines[::-1]:
        pl.semaphore_signal(barrier, inc=1, device_id=line(p), device_id_type=MESH)
    for p in planes:
        pl.semaphore_signal(barrier, inc=1, device_id=plane(p), device_id_type=MESH)

    loads = [
        pltpu.make_async_copy(src, dst, load_s.at[k])
        for k, (src, dst) in enumerate(
            ((text_hbm, text_ref), (audio_hbm, audio_ref), (image_hbm, image_ref))
        )
    ]
    for load in loads:
        load.start()
    loads[0].wait()
    v = text_ref[...].astype(jnp.float32)
    pair[0, b] = (v * inverse_radius(v)).astype(jnp.bfloat16)
    loads[1].wait()
    v = audio_ref[...].astype(jnp.float32)
    pair[1, b] = (v * inverse_radius(v)).astype(jnp.bfloat16)
    loads[2].wait()
    v = image_ref[...].astype(jnp.float32)
    img[a] = (v * inverse_radius(v)).astype(jnp.bfloat16)

    pl.semaphore_wait(barrier, A - 1 + B - 1)
    both = (0, 1)
    for m in both:
        for p in mates:
            go(pair.at[m, b], pair.at[m, b], pair_s.at[m * B + p], pair_r.at[m * B + b], plane(p))
    for p in lines:
        go(img.at[a], img.at[a], img_s.at[p], img_r.at[a], line(p))
    if step == 2:
        for m in both:
            go(pair.at[m, b], pair.at[m, b], fw_s.at[m * B + b], pair_r.at[m * B + b], (sibling, c))
    for m in both:
        for p in mates[::-1]:
            k = m * B + p
            arrive(pair.at[m, p], pair_s.at[k], pair_r.at[k], plane(p))
            if step == 2:
                go(pair.at[m, p], pair.at[m, p], fw_s.at[k], pair_r.at[k], (sibling, c))
    for p in lines:
        arrive(img.at[p], img_s.at[p], img_r.at[p], line(p))
    for m in both:
        for p in crossed:
            arrive(pair.at[m, p], fw_s.at[m * B + p], pair_r.at[m * B + p], (sibling, c))

    def image_ids(shape, axis):
        local = lax.broadcasted_iota(jnp.int32, shape, axis)
        return ((lax.div(local, n) * X + x) * R + r) * n + lax.rem(local, n)

    def pair_ids(shape, axis):
        local = lax.rem(lax.broadcasted_iota(jnp.int32, shape, axis), H)
        block = lax.div(local, n)
        block = lax.div(block, X) * C + a * X + lax.rem(block, X)
        return block * n + lax.rem(local, n)

    images = img[...].reshape(M, F)
    pairs = pair[...].reshape(Q, F)
    s_pi = logit_scale * contract(pairs, images, 1, 1)
    same_pi = image_ids((1, M), 1) == pair_ids((Q, 1), 0)
    diagonal = jnp.sum(jnp.where(same_pi, s_pi, 0.0), axis=0, keepdims=True)
    e_pi = jnp.exp(s_pi - logit_scale)
    text_row = jnp.sum(e_pi[:H], axis=0, keepdims=True)
    audio_row = jnp.sum(e_pi[H:], axis=0, keepdims=True)
    index = lax.broadcasted_iota(jnp.int32, (8, M), 0)
    stat_a[a] = jnp.where(index == 0, text_row, jnp.where(index == 1, audio_row, diagonal))
    for p in lines:
        go(stat_a.at[a], stat_a.at[a], sa_s.at[p], sa_r.at[a], line(p))
    e_ip = jnp.exp(logit_scale * contract(images, pairs, 1, 1) - logit_scale)
    column = jnp.sum(e_ip, axis=0, keepdims=True)
    pieces = [column[:, k : k + 128] for k in range(0, Q, 128)]
    pieces = pieces * max(1, 8 // len(pieces))
    stat_b[b] = jnp.concatenate(pieces, axis=0)
    for p in planes:
        go(stat_b.at[b], stat_b.at[b], sb_s.at[p], sb_r.at[b], plane(p))
    for p in planes:
        arrive(stat_b.at[p], sb_s.at[p], sb_r.at[p], plane(p))
    columns = stat_b[0]
    for p in range(1, B):
        columns = columns + stat_b[p]
    columns = jnp.concatenate([columns[k : k + 1] for k in range(Q // 128)], axis=1)
    inverse_c = 1.0 / columns
    inverse_c_tall = jnp.transpose(jnp.broadcast_to(inverse_c, (128, Q)))
    inverse_c_tall = jnp.concatenate([inverse_c_tall] * (M // 128), axis=1)
    loss_a[a] = jnp.broadcast_to(jnp.sum(jnp.log(columns), keepdims=True), (8, 128))
    for p in lines:
        go(loss_a.at[a], loss_a.at[a], la_s.at[p], la_r.at[a], line(p))

    for p in lines:
        arrive(stat_a.at[p], sa_s.at[p], sa_r.at[p], line(p))
    totals = stat_a[0]
    for p in range(1, A):
        totals = totals + stat_a[p]
    text_row, audio_row, diagonal = totals[0:1], totals[1:2], totals[2:3]
    loss_part = jnp.sum(jnp.log(text_row) + jnp.log(audio_row) - 2.0 * diagonal, keepdims=True)
    loss_b[b] = jnp.broadcast_to(loss_part, (8, 128))
    for p in planes:
        go(loss_b.at[b], loss_b.at[b], lb_s.at[p], lb_r.at[b], plane(p))
    inverse_text = jnp.broadcast_to(1.0 / text_row, (H, M))
    inverse_audio = jnp.broadcast_to(1.0 / audio_row, (H, M))
    w_pi = e_pi * (jnp.concatenate([inverse_text, inverse_audio], axis=0) + inverse_c_tall)
    w_pi = (w_pi - jnp.where(same_pi, 2.0, 0.0)).astype(jnp.bfloat16)
    for m in both:
        acc[m] = contract(w_pi[m * H : (m + 1) * H], images, 1, 0).reshape(B, n, F)
        for p in crossed:
            k = m * B + p
            part_p[m, p] = acc[m, p].astype(jnp.bfloat16)
            go(part_p.at[m, p], recv_h.at[m, p], ph_s.at[k], ph_r.at[k], (sibling, c))

    same_ip = image_ids((M, 1), 0) == pair_ids((1, Q), 1)
    inverse_rows = jnp.concatenate(
        [jnp.transpose(inverse_text), jnp.transpose(inverse_audio)], axis=1
    )
    w_ip = e_ip * (inverse_rows + inverse_c)
    w_ip = (w_ip - jnp.where(same_ip, 2.0, 0.0)).astype(jnp.bfloat16)
    part_i[...] = contract(w_ip, pairs, 1, 0).astype(jnp.bfloat16).reshape(A, n, F)
    for p in lines:
        go(part_i.at[p], recv_i.at[a], pi_s.at[p], pi_r.at[a], line(p))
    for m in both:
        for p in mates:
            k = m * B + p
            partial = acc[m, p]
            if step == 2:
                arrive(recv_h.at[m, p], ph_s.at[k], ph_r.at[k], (sibling, c))
                partial = partial + recv_h[m, p].astype(jnp.float32)
            part_p[m, p] = partial.astype(jnp.bfloat16)
            go(part_p.at[m, p], recv_p.at[m, b], pp_s.at[k], pp_r.at[m * B + b], plane(p))

    def finish(values_ref, out_ref, gradient):
        values = values_ref[...].astype(jnp.float32)
        inverse = inverse_radius(values)
        unit = values * inverse
        gradient = logit_scale * gradient
        inner = jnp.sum(unit * gradient, axis=-1, keepdims=True)
        out_ref[...] = (gradient - unit * inner) * inverse

    for m, values_ref, out_ref in ((0, text_ref, text_out), (1, audio_ref, audio_out)):
        pair_sum = acc[m, b]
        if step == 2:
            arrive(recv_h.at[m, b], ph_s.at[m * B + b], ph_r.at[m * B + b], (sibling, c))
            pair_sum = pair_sum + recv_h[m, b].astype(jnp.float32)
        for p in mates[::-1]:
            arrive(recv_p.at[m, p], pp_s.at[m * B + p], pp_r.at[m * B + p], plane(p))
            pair_sum = pair_sum + recv_p[m, p].astype(jnp.float32)
        finish(values_ref, out_ref, pair_sum)
    image_sum = part_i[a].astype(jnp.float32)
    for p in lines:
        arrive(recv_i.at[p], pi_s.at[p], pi_r.at[p], line(p))
        image_sum = image_sum + recv_i[p].astype(jnp.float32)
    finish(image_ref, image_out, image_sum)
    for p in lines:
        arrive(loss_a.at[p], la_s.at[p], la_r.at[p], line(p))
    for p in planes:
        arrive(loss_b.at[p], lb_s.at[p], lb_r.at[p], plane(p))
    total = loss_a[0]
    for p in range(1, A):
        total = total + loss_a[p]
    for p in range(B):
        total = total + loss_b[p]
    loss_out[0, 0] = jnp.max(total) / (4.0 * n * R * C) + logit_scale
    for one in sent:
        one.wait_send()


def write_back(a_ref, b_ref, c_ref, a_out, b_out, c_out, done):
    copies = [
        pltpu.make_async_copy(src, dst, done.at[k])
        for k, (src, dst) in enumerate(((a_ref, a_out), (b_ref, b_out), (c_ref, c_out)))
    ]
    for copy in copies:
        copy.start()
    for copy in copies:
        copy.wait()


def solution(mesh):
    R, C = mesh.shape["row"], mesh.shape["col"]
    X = 1
    while R * X < C // X and C % (2 * X) == 0:
        X *= 2
    A, B = C // X, R * X

    def shards(image, text, audio):
        n, F = image.shape
        M, Q = A * n, 2 * B * n
        vmem = pl.BlockSpec(memory_space=pltpu.VMEM)
        hbm = pl.BlockSpec(memory_space=pltpu.HBM)
        f32, bf16 = jnp.float32, jnp.bfloat16
        grad = pltpu.VMEM((n, F), f32)
        sem = pltpu.SemaphoreType.DMA
        sems = [sem((A,))] * 8 + [sem((2 * B,))] * 2 + [sem((B,))] * 4 + [sem((2 * B,))] * 5
        image_grad, text_grad, audio_grad, loss = pl.pallas_call(
            functools.partial(kernel, R, C, X, n, F),
            out_shape=(grad, grad, grad, jax.ShapeDtypeStruct((1, 1), f32)),
            in_specs=[hbm] * 3,
            out_specs=(vmem, vmem, vmem, pl.BlockSpec(memory_space=pltpu.SMEM)),
            scratch_shapes=[
                pltpu.VMEM((A, n, F), bf16),
                pltpu.VMEM((2, B, n, F), bf16),
                pltpu.VMEM((A, 8, M), f32),
                pltpu.VMEM((B, max(8, Q // 128), 128), f32),
                pltpu.VMEM((A, 8, 128), f32),
                pltpu.VMEM((B, 8, 128), f32),
                pltpu.VMEM((A, n, F), bf16),
                pltpu.VMEM((A, n, F), bf16),
                pltpu.VMEM((2, B, n, F), f32),
                pltpu.VMEM((2, B, n, F), bf16),
                pltpu.VMEM((2, B, n, F), bf16),
                pltpu.VMEM((2, B, n, F), bf16),
            ]
            + sems
            + [pltpu.VMEM((n, F), bf16)] * 3
            + [sem((3,))],
            compiler_params=pltpu.CompilerParams(
                collective_id=0, has_side_effects=True, vmem_limit_bytes=67043328 - 13 * n * F
            ),
        )(image, text, audio)
        full = jax.ShapeDtypeStruct((n, F), f32)
        image_grad, text_grad, audio_grad = pl.pallas_call(
            write_back,
            out_shape=(full,) * 3,
            in_specs=[vmem] * 3,
            out_specs=(hbm,) * 3,
            scratch_shapes=[sem((3,))],
            compiler_params=pltpu.CompilerParams(vmem_limit_bytes=1 << 20),
        )(image_grad, text_grad, audio_grad)
        return image_grad, text_grad, audio_grad, loss.reshape(())

    first, second = P(("col", "row"), None), P(("row", "col"), None)
    return jax.shard_map(
        shards,
        mesh=mesh,
        in_specs=(first, second, second),
        out_specs=(first, second, second, P()),
        check_vma=False,
    )
```

```python
import functools

import jax
import jax.numpy as jnp
from jax import lax
from jax.experimental import pallas as pl
from jax.experimental.pallas import tpu as pltpu
from jax.sharding import PartitionSpec as P

MESH = pl.DeviceIdType.MESH
logit_scale = 20.0
epsilon = 1e-06


def inverse_radius(values):
    return lax.rsqrt(jnp.sum(values * values, axis=-1, keepdims=True) + epsilon)


def contract(left, right, left_dim, right_dim):
    return lax.dot_general(
        left, right, (((left_dim,), (right_dim,)), ((), ())), preferred_element_type=jnp.float32
    )


def kernel(
    R, C, X, n, F,
    image_hbm, text_hbm, audio_hbm,
    image_out, text_out, audio_out, loss_out,
    img, pair, stat_a, stat_b, loss_a, loss_b,
    part_i, recv_i, acc, part_p, recv_h, recv_p,
    img_s, img_r, sa_s, sa_r, la_s, la_r, pi_s, pi_r,
    pair_s, pair_r, sb_s, sb_r, lb_s, lb_r, ph_s, ph_r, pp_s, pp_r, fw_s,
    image_ref, text_ref, audio_ref, load_s,
):
    r = lax.axis_index("row")
    c = lax.axis_index("col")
    A, B = C // X, R * X
    M, H = A * n, B * n
    Q = 2 * H
    a = lax.div(c, X)
    x = lax.rem(c, X)
    b = r * X + x
    step = 2 if R % 2 == 0 else 1
    sibling = r + 1 - 2 * lax.rem(r, 2)
    side = 2 * lax.rem(a, 2) - 1
    far_first = sorted(range(1, A), key=lambda k: abs(2 * k - A))
    lines = [lax.rem(a + side * k + A, A) for k in far_first]
    planes = [lax.rem(b + k, B) for k in range(1, B)]
    turns = [
        (lax.rem(r + i, R), lax.rem(x + j, X))
        for i in range(R - step, -1, -step)
        for j in range(X - 1, -1, -1)
    ]
    mates = [p * X + q for p, q in turns[:-1]]
    crossed = [(p + sibling - r) * X + q for p, q in turns] if step == 2 else []

    def line(p):
        return (r, p * X + x)

    def plane(p):
        return (lax.div(p, X), a * X + lax.rem(p, X))

    def copy(src, dst, send, recv, device):
        return pltpu.make_async_remote_copy(
            src_ref=src, dst_ref=dst, send_sem=send, recv_sem=recv,
            device_id=device, device_id_type=MESH,
        )

    sent = []

    def go(*args):
        one = copy(*args)
        one.start()
        sent.append(one)

    def arrive(dst, send, recv, device):
        copy(dst, dst, send, recv, device).wait_recv()

    barrier = pltpu.get_barrier_semaphore()
    for p in lines[::-1]:
        pl.semaphore_signal(barrier, inc=1, device_id=line(p), device_id_type=MESH)
    for p in planes:
        pl.semaphore_signal(barrier, inc=1, device_id=plane(p), device_id_type=MESH)

    loads = [
        pltpu.make_async_copy(src, dst, load_s.at[k])
        for k, (src, dst) in enumerate(
            ((text_hbm, text_ref), (audio_hbm, audio_ref), (image_hbm, image_ref))
        )
    ]
    for load in loads:
        load.start()
    loads[0].wait()
    v = text_ref[...].astype(jnp.float32)
    pair[0, b] = (v * inverse_radius(v)).astype(jnp.bfloat16)
    loads[1].wait()
    v = audio_ref[...].astype(jnp.float32)
    pair[1, b] = (v * inverse_radius(v)).astype(jnp.bfloat16)
    loads[2].wait()
    v = image_ref[...].astype(jnp.float32)
    img[a] = (v * inverse_radius(v)).astype(jnp.bfloat16)

    pl.semaphore_wait(barrier, A - 1 + B - 1)
    both = (0, 1)
    for m in both:
        for p in mates:
            go(pair.at[m, b], pair.at[m, b], pair_s.at[m * B + p], pair_r.at[m * B + b], plane(p))
    for p in lines:
        go(img.at[a], img.at[a], img_s.at[p], img_r.at[a], line(p))
    if step == 2:
        for m in both:
            go(pair.at[m, b], pair.at[m, b], fw_s.at[m * B + b], pair_r.at[m * B + b], (sibling, c))
    for m in both:
        for p in mates[::-1]:
            k = m * B + p
            arrive(pair.at[m, p], pair_s.at[k], pair_r.at[k], plane(p))
            if step == 2:
                go(pair.at[m, p], pair.at[m, p], fw_s.at[k], pair_r.at[k], (sibling, c))
    for p in lines:
        arrive(img.at[p], img_s.at[p], img_r.at[p], line(p))
    for m in both:
        for p in crossed:
            arrive(pair.at[m, p], fw_s.at[m * B + p], pair_r.at[m * B + p], (sibling, c))

    def image_ids(shape, axis):
        local = lax.broadcasted_iota(jnp.int32, shape, axis)
        return ((lax.div(local, n) * X + x) * R + r) * n + lax.rem(local, n)

    def pair_ids(shape, axis):
        local = lax.rem(lax.broadcasted_iota(jnp.int32, shape, axis), H)
        block = lax.div(local, n)
        block = lax.div(block, X) * C + a * X + lax.rem(block, X)
        return block * n + lax.rem(local, n)

    images = img[...].reshape(M, F)
    pairs = pair[...].reshape(Q, F)
    s_pi = logit_scale * contract(pairs, images, 1, 1)
    same_pi = image_ids((1, M), 1) == pair_ids((Q, 1), 0)
    diagonal = jnp.sum(jnp.where(same_pi, s_pi, 0.0), axis=0, keepdims=True)
    e_pi = jnp.exp(s_pi - logit_scale)
    text_row = jnp.sum(e_pi[:H], axis=0, keepdims=True)
    audio_row = jnp.sum(e_pi[H:], axis=0, keepdims=True)
    index = lax.broadcasted_iota(jnp.int32, (8, M), 0)
    stat_a[a] = jnp.where(index == 0, text_row, jnp.where(index == 1, audio_row, diagonal))
    for p in lines:
        go(stat_a.at[a], stat_a.at[a], sa_s.at[p], sa_r.at[a], line(p))
    e_ip = jnp.exp(logit_scale * contract(images, pairs, 1, 1) - logit_scale)
    column = jnp.sum(e_ip, axis=0, keepdims=True)
    pieces = [column[:, k : k + 128] for k in range(0, Q, 128)]
    pieces = pieces * max(1, 8 // len(pieces))
    stat_b[b] = jnp.concatenate(pieces, axis=0)
    for p in planes:
        go(stat_b.at[b], stat_b.at[b], sb_s.at[p], sb_r.at[b], plane(p))
    for p in planes:
        arrive(stat_b.at[p], sb_s.at[p], sb_r.at[p], plane(p))
    columns = stat_b[0]
    for p in range(1, B):
        columns = columns + stat_b[p]
    columns = jnp.concatenate([columns[k : k + 1] for k in range(Q // 128)], axis=1)
    inverse_c = 1.0 / columns
    inverse_c_tall = jnp.transpose(jnp.broadcast_to(inverse_c, (128, Q)))
    inverse_c_tall = jnp.concatenate([inverse_c_tall] * (M // 128), axis=1)
    loss_a[a] = jnp.broadcast_to(jnp.sum(jnp.log(columns), keepdims=True), (8, 128))
    for p in lines:
        go(loss_a.at[a], loss_a.at[a], la_s.at[p], la_r.at[a], line(p))

    for p in lines:
        arrive(stat_a.at[p], sa_s.at[p], sa_r.at[p], line(p))
    totals = stat_a[0]
    for p in range(1, A):
        totals = totals + stat_a[p]
    text_row, audio_row, diagonal = totals[0:1], totals[1:2], totals[2:3]
    loss_part = jnp.sum(jnp.log(text_row) + jnp.log(audio_row) - 2.0 * diagonal, keepdims=True)
    loss_b[b] = jnp.broadcast_to(loss_part, (8, 128))
    for p in planes:
        go(loss_b.at[b], loss_b.at[b], lb_s.at[p], lb_r.at[b], plane(p))
    inverse_text = jnp.broadcast_to(1.0 / text_row, (H, M))
    inverse_audio = jnp.broadcast_to(1.0 / audio_row, (H, M))
    w_pi = e_pi * (jnp.concatenate([inverse_text, inverse_audio], axis=0) + inverse_c_tall)
    w_pi = (w_pi - jnp.where(same_pi, 2.0, 0.0)).astype(jnp.bfloat16)
    same_ip = image_ids((M, 1), 0) == pair_ids((1, Q), 1)
    inverse_rows = jnp.concatenate(
        [jnp.transpose(inverse_text), jnp.transpose(inverse_audio)], axis=1
    )
    w_ip = e_ip * (inverse_rows + inverse_c)
    w_ip = (w_ip - jnp.where(same_ip, 2.0, 0.0)).astype(jnp.bfloat16)
    part_i[...] = contract(w_ip, pairs, 1, 0).astype(jnp.bfloat16).reshape(A, n, F)
    for p in lines:
        go(part_i.at[p], recv_i.at[a], pi_s.at[p], pi_r.at[a], line(p))
    for m in both:
        acc[m] = contract(w_pi[m * H : (m + 1) * H], images, 1, 0).reshape(B, n, F)
        for p in crossed:
            k = m * B + p
            part_p[m, p] = acc[m, p].astype(jnp.bfloat16)
            go(part_p.at[m, p], recv_h.at[m, p], ph_s.at[k], ph_r.at[k], (sibling, c))
    for m in both:
        for p in mates:
            k = m * B + p
            partial = acc[m, p]
            if step == 2:
                arrive(recv_h.at[m, p], ph_s.at[k], ph_r.at[k], (sibling, c))
                partial = partial + recv_h[m, p].astype(jnp.float32)
            part_p[m, p] = partial.astype(jnp.bfloat16)
            go(part_p.at[m, p], recv_p.at[m, b], pp_s.at[k], pp_r.at[m * B + b], plane(p))

    def finish(values_ref, out_ref, gradient):
        values = values_ref[...].astype(jnp.float32)
        inverse = inverse_radius(values)
        unit = values * inverse
        gradient = logit_scale * gradient
        inner = jnp.sum(unit * gradient, axis=-1, keepdims=True)
        out_ref[...] = (gradient - unit * inner) * inverse

    for m, values_ref, out_ref in ((0, text_ref, text_out), (1, audio_ref, audio_out)):
        pair_sum = acc[m, b]
        if step == 2:
            arrive(recv_h.at[m, b], ph_s.at[m * B + b], ph_r.at[m * B + b], (sibling, c))
            pair_sum = pair_sum + recv_h[m, b].astype(jnp.float32)
        for p in mates[::-1]:
            arrive(recv_p.at[m, p], pp_s.at[m * B + p], pp_r.at[m * B + p], plane(p))
            pair_sum = pair_sum + recv_p[m, p].astype(jnp.float32)
        finish(values_ref, out_ref, pair_sum)
    image_sum = part_i[a].astype(jnp.float32)
    for p in lines:
        arrive(recv_i.at[p], pi_s.at[p], pi_r.at[p], line(p))
        image_sum = image_sum + recv_i[p].astype(jnp.float32)
    finish(image_ref, image_out, image_sum)
    for p in lines:
        arrive(loss_a.at[p], la_s.at[p], la_r.at[p], line(p))
    for p in planes:
        arrive(loss_b.at[p], lb_s.at[p], lb_r.at[p], plane(p))
    total = loss_a[0]
    for p in range(1, A):
        total = total + loss_a[p]
    for p in range(B):
        total = total + loss_b[p]
    loss_out[0, 0] = jnp.max(total) / (4.0 * n * R * C) + logit_scale
    for one in sent:
        one.wait_send()


def write_back(a_ref, b_ref, c_ref, a_out, b_out, c_out, done):
    copies = [
        pltpu.make_async_copy(src, dst, done.at[k])
        for k, (src, dst) in enumerate(((a_ref, a_out), (b_ref, b_out), (c_ref, c_out)))
    ]
    for copy in copies:
        copy.start()
    for copy in copies:
        copy.wait()


def solution(mesh):
    R, C = mesh.shape["row"], mesh.shape["col"]
    X = 1
    while R * X < C // X and C % (2 * X) == 0:
        X *= 2
    A, B = C // X, R * X

    def shards(image, text, audio):
        n, F = image.shape
        M, Q = A * n, 2 * B * n
        vmem = pl.BlockSpec(memory_space=pltpu.VMEM)
        hbm = pl.BlockSpec(memory_space=pltpu.HBM)
        f32, bf16 = jnp.float32, jnp.bfloat16
        grad = pltpu.VMEM((n, F), f32)
        sem = pltpu.SemaphoreType.DMA
        sems = [sem((A,))] * 8 + [sem((2 * B,))] * 2 + [sem((B,))] * 4 + [sem((2 * B,))] * 5
        image_grad, text_grad, audio_grad, loss = pl.pallas_call(
            functools.partial(kernel, R, C, X, n, F),
            out_shape=(grad, grad, grad, jax.ShapeDtypeStruct((1, 1), f32)),
            in_specs=[hbm] * 3,
            out_specs=(vmem, vmem, vmem, pl.BlockSpec(memory_space=pltpu.SMEM)),
            scratch_shapes=[
                pltpu.VMEM((A, n, F), bf16),
                pltpu.VMEM((2, B, n, F), bf16),
                pltpu.VMEM((A, 8, M), f32),
                pltpu.VMEM((B, max(8, Q // 128), 128), f32),
                pltpu.VMEM((A, 8, 128), f32),
                pltpu.VMEM((B, 8, 128), f32),
                pltpu.VMEM((A, n, F), bf16),
                pltpu.VMEM((A, n, F), bf16),
                pltpu.VMEM((2, B, n, F), f32),
                pltpu.VMEM((2, B, n, F), bf16),
                pltpu.VMEM((2, B, n, F), bf16),
                pltpu.VMEM((2, B, n, F), bf16),
            ]
            + sems
            + [pltpu.VMEM((n, F), bf16)] * 3
            + [sem((3,))],
            compiler_params=pltpu.CompilerParams(
                collective_id=0, has_side_effects=True, vmem_limit_bytes=67043328 - 13 * n * F
            ),
        )(image, text, audio)
        full = jax.ShapeDtypeStruct((n, F), f32)
        image_grad, text_grad, audio_grad = pl.pallas_call(
            write_back,
            out_shape=(full,) * 3,
            in_specs=[vmem] * 3,
            out_specs=(hbm,) * 3,
            scratch_shapes=[sem((3,))],
            compiler_params=pltpu.CompilerParams(vmem_limit_bytes=1 << 20),
        )(image_grad, text_grad, audio_grad)
        return image_grad, text_grad, audio_grad, loss.reshape(())

    first, second = P(("col", "row"), None), P(("row", "col"), None)
    return jax.shard_map(
        shards,
        mesh=mesh,
        in_specs=(first, second, second),
        out_specs=(first, second, second, P()),
        check_vma=False,
    )
```
